256 devices in a mesh: ta: 64 (over y, z_lo, x, core), site: 4 (over z_hi).
Axes of the slice: x: 4, y: 4, z: 8 (z_hi: 4, z_lo: 2; z = z_hi * 2 + z_lo), core: 2. Of those that a mesh axis runs over, the one named last changes fastest.
Arguments:
- eigenvectors: bfloat16 [128, 192, 3, 4, 256], P('ta', None, None, 'site'), parts along dimension 0, may hold values from -6 to 6
- gauge_links: bfloat16 [128, 3, 3, 3, 4, 256], P('ta', None, None, None, 'site'), parts along dimension 0, may hold values from -2.5 to 2.5
- displacements: int32 [2, 3], replicated, may hold values from 0 to 3, as said below
- block_rows: int32 [4], replicated, may hold values from 0 to 191
Outputs:
- elementals: float32 [128, 4, 192, 384], P('ta', None, 'site'), parts along dimension 0
The draws below stay inside these ranges and needn't reach their ends.
There are 64 independent parts, one for each index of `ta`. The reference program is written for one: setup_inputs(seed, part) draws one part's arguments, and reference() takes and returns one part's arrays. A program takes and returns all parts, laid end to end along the dimension named above; an argument that names none is the same for every part. Nothing has to cross between parts.
Inputs may be any that keep to these rules, and one draw needn't show every extreme that they name: `displacements`: each combination displaces at least one of its three vectors along the third dimension.
All inputs are finite; a program needn't handle non-finite values.
Results may differ from the reference program's by a relative error of at most 0.012.
Values may be sent and summed in bfloat16 or wider, within the bound.
A program may use at most 64 MiB of HBM per device.

```python
import math
import jax
import jax.numpy as jnp
from jax import lax

NV = 192
IB = 4
NCOMB = 2
LX = 16
LZ = 4
LXY = 256
VOL = 1024


def draw_displacements(key, part):
    directions = jax.random.randint(key, (NCOMB, 3), 0, 4)
    chosen_slot = jax.random.randint(jax.random.fold_in(key, 7), (NCOMB,), 0, 3)
    forced = jnp.arange(3)[None, :] == chosen_slot[:, None]
    return jnp.where(forced, 3, directions).astype(jnp.int32)


def touch_ends(values, rng, low, high):
    shape = values.shape
    spot = [jax.random.randint(jax.random.fold_in(rng, axis), (), 0, shape[axis]) for axis in range(len(shape))]
    values = values.at[tuple(spot)].set(low)
    longest = shape.index(max(shape))
    spot[longest] = (spot[longest] + 1) % shape[longest]
    return values.at[tuple(spot)].set(high)


def block_scale(rng, extent, split, smallest, high):
    gain = 1.0
    for position, parts in split:
        heights = jax.random.uniform(jax.random.fold_in(jax.random.fold_in(rng, 6), position), (parts,), jnp.float32, smallest / len(split), high / len(split))
        gain = gain * jnp.repeat(jnp.exp(heights), extent[position] // parts).reshape((-1,) + (1,) * (len(extent) - 1 - position))
    return gain


def gaussian(rng, extent, deviation, reach, pieces=(), kind=jnp.bfloat16):
    values = jax.random.normal(rng, extent, jnp.float32) * deviation
    if len(pieces) > 0:
        values = block_scale(rng, extent, pieces, -0.22, 0.18) * values
    return jnp.clip(values, min=-reach, max=reach).astype(kind)


def setup_inputs(seed: int = 0, part: int = 0) -> dict:
    streams_of = jax.random.split(jax.random.key(seed), 5)
    part_splits = jax.random.split(jax.random.fold_in(streams_of[4], part), 5)
    eigenvectors = gaussian(part_splits[0], (2, NV, 3, LZ, LXY), 1.0, 6.0, ((3, 4),))
    gauge_links = gaussian(part_splits[1], (2, 3, 3, 3, LZ, LXY), 6 ** -0.5, 2.5, ((4, 4),))
    displacements = draw_displacements(jax.random.fold_in(streams_of[4], 71), part)
    block_rows = touch_ends(jax.random.randint(streams_of[3], (IB,), 0, NV), jax.random.fold_in(streams_of[3], 1), 0, NV - 1).astype(jnp.int32)
    return {"eigenvectors": eigenvectors, "gauge_links": gauge_links, "displacements": displacements, "block_rows": block_rows}


def neighbours(vectors, direction, width_x):

    def along_x(values):
        shaped = values.reshape(values.shape[:-1] + (-1, width_x))
        return jnp.roll(shaped, -1, axis=-1).reshape(values.shape)

    def along_y(values):
        shaped = values.reshape(values.shape[:-1] + (-1, width_x))
        return jnp.roll(shaped, -1, axis=-2).reshape(values.shape)

    def along_z(values):
        return jnp.roll(values, -1, axis=3)
    return lax.switch(direction, [lambda values: values, along_x, along_y, along_z], vectors)

def displace(vectors, links, direction, width_x):
    moved = neighbours(vectors, direction, width_x).astype(jnp.float32)
    chosen = lax.dynamic_index_in_dim(links, jnp.maximum(direction - 1, 0), axis=1, keepdims=False).astype(jnp.float32)
    identity = jnp.eye(3, dtype=jnp.float32)[:, :, None, None]
    resting = direction == 0
    link_re = jnp.where(resting, identity, chosen[0])
    link_im = jnp.where(resting, jnp.zeros_like(chosen[1]), chosen[1])

    def multiply(matrix, component):
        return jnp.einsum('abzs,nbzs->nazs', matrix, component)
    out_re = multiply(link_re, moved[0]) - multiply(link_im, moved[1])
    out_im = multiply(link_re, moved[1]) + multiply(link_im, moved[0])
    return jnp.stack([out_re, out_im]).astype(jnp.bfloat16)

def cross_triple(left_field, mid_field):
    left_re = left_field[0].astype(jnp.float32)[:, None]
    left_im = left_field[1].astype(jnp.float32)[:, None]
    mid_re = mid_field[0].astype(jnp.float32)[None]
    mid_im = mid_field[1].astype(jnp.float32)[None]

    def product_re(first_color, second_color):
        return left_re[:, :, first_color] * mid_re[:, :, second_color] - left_im[:, :, first_color] * mid_im[:, :, second_color]

    def product_im(first_color, second_color):
        return left_re[:, :, first_color] * mid_im[:, :, second_color] + left_im[:, :, first_color] * mid_re[:, :, second_color]
    orders = ((1, 2), (2, 0), (0, 1))
    cross_re = jnp.stack([product_re(one, two) - product_re(two, one) for one, two in orders], axis=2)
    cross_im = jnp.stack([product_im(one, two) - product_im(two, one) for one, two in orders], axis=2)
    return jnp.stack([cross_re, cross_im], axis=2).astype(jnp.bfloat16)

def contract_sites(crossed, right_field):
    rows_count = crossed.shape[0] * crossed.shape[1]
    left = crossed.reshape(rows_count, -1)
    count_k = right_field.shape[1]
    right_re = right_field[0].reshape(count_k, -1)
    right_im = right_field[1].reshape(count_k, -1)
    upper = jnp.concatenate([right_re, -right_im], axis=1)
    lower = jnp.concatenate([right_im, right_re], axis=1)
    right = jnp.concatenate([upper, lower], axis=0)
    result = lax.dot_general(left, right, (((1,), (1,)), ((), ())), preferred_element_type=jnp.float32)
    return result.reshape(crossed.shape[0], crossed.shape[1], 2 * count_k)

def reference(eigenvectors, gauge_links, displacements, block_rows):
    picked = jnp.take(eigenvectors, block_rows, axis=1)
    results = []
    for combo in range(NCOMB):
        left_field = displace(picked, gauge_links, displacements[combo, 0], LX)
        mid_field = displace(eigenvectors, gauge_links, displacements[combo, 1], LX)
        right_field = displace(eigenvectors, gauge_links, displacements[combo, 2], LX)
        results.append(contract_sites(cross_triple(left_field, mid_field), right_field))
    scale = 1.0 / math.sqrt(24.0 * VOL)
    return jnp.stack(results) * scale
```

```python
import functools
import math

import jax
import jax.numpy as jnp
from jax import lax
from jax.experimental import pallas as pl
from jax.experimental.pallas import tpu as pltpu
from jax.sharding import PartitionSpec as P

LX = 16
RING = 4
LINK_ROWS = 24
NT = (((1,), (1,)), ((), ()))


def shift_matrix(moved_x, moved_y, sites):
    here = lax.broadcasted_iota(jnp.int32, (1, sites), 1)
    x, y = here % LX, here // LX
    rows = sites // LX
    there = ((y + moved_y + rows) % rows) * LX + (x + moved_x + LX) % LX
    source = lax.broadcasted_iota(jnp.int32, (sites, sites), 0)
    return jnp.where(source == there, 1.0, 0.0).astype(jnp.bfloat16)


def as_int(condition):
    return jnp.where(condition, 1, 0)


def kernel(scale, disp, rows, psi, links, out, g, jb, sb, s32, u32, l32, w32, j32, x, perm,
           local_sem, send, recv, small_send, small_recv):
    me = lax.axis_index("site")
    after, behind, across = (me + 1) % RING, (me + 3) % RING, (me + 2) % RING
    block = jb.shape[3]
    sites = jb.shape[4]

    def own(offset):
        return (me + offset) % RING

    fills = []
    for chunk in range(RING):
        fills.append(pltpu.make_async_copy(
            psi.at[:, :, pl.ds(chunk * block, block), :], g.at[0, chunk], local_sem.at[chunk]))
    fills.append(pltpu.make_async_copy(
        psi.at[:, :, pl.ds(pl.multiple_of(me * block, block), block), :], jb.at[0], local_sem.at[RING]))
    for fill in fills:
        fill.start()

    barrier = pltpu.get_barrier_semaphore()
    for peer in (after, behind, across):
        pl.semaphore_signal(barrier, inc=1, device_id={"site": peer})
    pl.semaphore_wait(barrier, 3)
    for fill in fills:
        fill.wait()

    def carry(lane, number, source, target, peer):
        return pltpu.make_async_remote_copy(
            src_ref=source, dst_ref=target,
            send_sem=send.at[lane, number], recv_sem=recv.at[lane, number],
            device_id={"site": peer})

    up = [
        carry(0, 0, g.at[0, own(2)], g.at[3, own(2)], after),
        carry(0, 1, g.at[0, own(1)], jb.at[3], after),
        carry(0, 2, g.at[3, own(1)], jb.at[2], after),
        carry(0, 3, g.at[0, own(0)], g.at[3, own(0)], after),
        carry(0, 4, g.at[0, own(3)], g.at[3, own(3)], after),
        carry(0, 5, jb.at[3], g.at[2, own(0)], after),
    ]
    down = [
        carry(1, 0, g.at[0, own(3)], jb.at[1], behind),
        carry(1, 1, g.at[0, own(0)], g.at[1, own(0)], behind),
        carry(1, 2, g.at[0, own(1)], g.at[1, own(1)], behind),
        carry(1, 3, g.at[0, own(2)], g.at[1, own(2)], behind),
        carry(1, 4, jb.at[1], g.at[2, own(0)], behind),
        carry(1, 5, g.at[1, own(1)], g.at[2, own(1)], behind),
    ]
    up[0].start()
    down[0].start()
    up[1].start()
    down[1].start()

    s32[...] = jnp.zeros_like(s32)
    for direction in range(3):
        for a in range(3):
            for b in range(3):
                at = direction * LINK_ROWS + (a * 3 + b) * 2
                s32[at:at + 2] = links[direction, a, b].astype(jnp.float32)
    vectors = RING * block
    number = lax.broadcasted_iota(jnp.int32, (LINK_ROWS, vectors), 0)
    column = lax.broadcasted_iota(jnp.int32, (LINK_ROWS, vectors), 1)
    wanted = jnp.zeros((LINK_ROWS, vectors), jnp.int32)
    for i in range(4):
        wanted = jnp.where(number % 4 == i, rows[i], wanted)
    found = column == wanted
    picked = jnp.zeros((LINK_ROWS, sites), jnp.float32)
    for q in range(2):
        for c in range(3):
            pick = jnp.where(found & (number // 4 == q * 3 + c), 1.0, 0.0).astype(jnp.bfloat16)
            whole = jnp.concatenate([g[0, chunk, q, c] for chunk in range(RING)], axis=0)
            picked += jnp.dot(pick, whole, preferred_element_type=jnp.float32)
    s32[3 * LINK_ROWS:4 * LINK_ROWS] = picked
    sb[0] = s32[...].astype(jnp.bfloat16)
    small = []
    for k, (slot, peer) in enumerate(((3, after), (1, behind), (2, across))):
        small.append(pltpu.make_async_remote_copy(
            src_ref=sb.at[0], dst_ref=sb.at[slot],
            send_sem=small_send.at[k], recv_sem=small_recv.at[k],
            device_id={"site": peer}))
        small[-1].start()

    for m in range(2):
        d1, d2, d3 = disp[m, 0], disp[m, 1], disp[m, 2]
        back_x, back_y = as_int(d3 == 1), as_int(d3 == 2)
        perm[m, 0] = shift_matrix(-back_x, -back_y, sites)
        perm[m, 1] = shift_matrix(as_int(d2 == 1) - back_x, as_int(d2 == 2) - back_y, sites)
        perm[m, 2] = shift_matrix(as_int(d1 == 1) - back_x, as_int(d1 == 2) - back_y, sites)

    up[0].wait_recv()
    up[2].start()
    up[3].start()
    down[0].wait_recv()
    down[2].start()
    up[1].wait_recv()
    up[4].start()
    up[5].start()
    down[1].wait_recv()
    down[3].start()
    down[4].start()
    down[5].start()
    for message in small:
        message.wait_recv()
    up[2].wait_recv()
    for slot in range(1, RING):
        g[slot, me] = jb[slot]

    def build(step, carried):
        slot, m = step // 2, step % 2
        d1, d2, d3 = disp[m, 0], disp[m, 1], disp[m, 2]
        base = (slot + RING - as_int(d3 == 3)) % RING
        mid = (base + as_int(d2 == 3)) % RING
        left = (base + as_int(d1 == 3)) % RING
        moved = jnp.dot(sb[base], perm[m, 0], preferred_element_type=jnp.float32)
        entry = lax.broadcasted_iota(jnp.int32, (LINK_ROWS, sites), 0)
        identity = jnp.where((entry == 0) | (entry == 8) | (entry == 16), 1.0, 0.0)
        for k, d in enumerate((d1, d2, d3)):
            chosen = identity
            for direction in range(3):
                candidate = moved[direction * LINK_ROWS:(direction + 1) * LINK_ROWS]
                chosen = jnp.where(d == direction + 1, candidate, chosen)
            u32[k] = chosen
        l32[...] = scale * jnp.dot(
            sb[left, 3 * LINK_ROWS:4 * LINK_ROWS, :], perm[m, 2], preferred_element_type=jnp.float32)
        j32[...] = jnp.dot(
            jb[mid].reshape(6 * block, sites), perm[m, 1],
            preferred_element_type=jnp.float32).reshape(j32.shape)

        def link(k, a, b):
            at = (a * 3 + b) * 2
            return (u32[k, at:at + 1, :], u32[k, at + 1:at + 2, :])

        def times(one, two):
            return (one[0] * two[0] - one[1] * two[1], one[0] * two[1] + one[1] * two[0])

        def plus(one, two):
            return (one[0] + two[0], one[1] + two[1])

        def minus(one, two):
            return (one[0] - two[0], one[1] - two[1])

        source = [(l32[4 * b:4 * b + 4, :], l32[12 + 4 * b:16 + 4 * b, :]) for b in range(3)]
        lefts = []
        for a in range(3):
            total = times(source[0], link(0, a, 0))
            for b in (1, 2):
                total = plus(total, times(source[b], link(0, a, b)))
            lefts.append(total)
        for d in range(3):
            triple = []
            for b in range(3):
                one, two = (b + 1) % 3, (b + 2) % 3
                triple.append(minus(times(lefts[two], link(2, one, d)), times(lefts[one], link(2, two, d))))
            for e in range(3):
                total = times(triple[0], link(1, 0, e))
                for b in (1, 2):
                    total = plus(total, times(triple[b], link(1, b, e)))
                w32[d, e, 0, 0:4, :] = total[0]
                w32[d, e, 1, 0:4, :] = total[1]

        for half in range(sites // 128):
            lanes = slice(half * 128, half * 128 + 128)
            re = [j32[e, :, lanes] for e in range(3)]
            im = [j32[3 + e, :, lanes] for e in range(3)]
            for d in range(3):
                for i in range(4):
                    total = None
                    for e in range(3):
                        w = (w32[d, e, 0, i:i + 1, lanes], w32[d, e, 1, i:i + 1, lanes])
                        term = times((re[e], im[e]), w)
                        total = term if total is None else plus(total, term)
                    place = slice(d * sites + half * 128, d * sites + half * 128 + 128)
                    for q in range(2):
                        x[slot, q, m, i * block:(i + 1) * block, place] = total[q].astype(jnp.bfloat16)
        return carried

    lax.fori_loop(0, 2 * RING, build, 0)

    def contract(slot):
        first, second = [], []
        for c in range(3):
            re = [g[slot, chunk, 0, c] for chunk in range(RING)]
            im = [g[slot, chunk, 1, c] for chunk in range(RING)]
            first.append(jnp.concatenate(re + im, axis=0))
            second.append(jnp.concatenate([-part for part in im] + re, axis=0))
        total = None
        for q, parts in enumerate((first, second)):
            left = x[slot, q].reshape(8 * block, 3 * sites)
            product = lax.dot_general(
                left, jnp.concatenate(parts, axis=1), NT, preferred_element_type=jnp.float32)
            total = product if total is None else total + product
        return total.reshape(out.shape)

    out[...] = contract(0)
    for k in (2, 3):
        down[k].wait_recv()
    out[...] += contract(1)
    for k in (3, 4):
        up[k].wait_recv()
    out[...] += contract(3)
    up[5].wait_recv()
    down[4].wait_recv()
    down[5].wait_recv()
    out[...] += contract(2)
    for copy in up + down + small:
        copy.wait_send()


def on_device(eigenvectors, gauge_links, displacements, block_rows):
    psi = jnp.transpose(eigenvectors[:, :, :, 0, :], (0, 2, 1, 3))
    links = jnp.transpose(gauge_links[:, :, :, :, 0, :], (1, 2, 3, 0, 4))
    _, colors, vectors, sites = psi.shape
    block = vectors // RING
    scale = 1.0 / math.sqrt(24.0 * sites * RING)
    f32, bf16 = jnp.float32, jnp.bfloat16
    vmem = pl.BlockSpec(memory_space=pltpu.VMEM)
    smem = pl.BlockSpec(memory_space=pltpu.SMEM)
    return pl.pallas_call(
        functools.partial(kernel, scale),
        out_shape=jax.ShapeDtypeStruct((2, 4, block, 2 * vectors), f32),
        in_specs=[smem, smem, pl.BlockSpec(memory_space=pl.ANY), vmem],
        out_specs=vmem,
        scratch_shapes=[
            pltpu.VMEM((RING, RING, 2, 3, block, sites), bf16),
            pltpu.VMEM((RING, 2, 3, block, sites), bf16),
            pltpu.VMEM((RING, 4 * LINK_ROWS, sites), bf16),
            pltpu.VMEM((4 * LINK_ROWS, sites), f32),
            pltpu.VMEM((3, LINK_ROWS, sites), f32),
            pltpu.VMEM((LINK_ROWS, sites), f32),
            pltpu.VMEM((3, 3, 2, 8, sites), f32),
            pltpu.VMEM((6, block, sites), f32),
            pltpu.VMEM((RING, 2, 2, 4 * block, 3 * sites), bf16),
            pltpu.VMEM((2, 3, sites, sites), bf16),
            pltpu.SemaphoreType.DMA((RING + 1,)),
            pltpu.SemaphoreType.DMA((2, 6)),
            pltpu.SemaphoreType.DMA((2, 6)),
            pltpu.SemaphoreType.DMA((3,)),
            pltpu.SemaphoreType.DMA((3,)),
        ],
        compiler_params=pltpu.CompilerParams(
            collective_id=0, has_side_effects=True, vmem_limit_bytes=40 * 1024 * 1024),
    )(displacements, block_rows, psi, links)


def solution(mesh):
    return jax.shard_map(
        on_device,
        mesh=mesh,
        in_specs=(
            P("ta", None, None, "site", None),
            P("ta", None, None, None, "site", None),
            P(),
            P(),
        ),
        out_specs=P("ta", None, "site", None),
        check_vma=False,
    )
```

```python
import functools
import math

import jax
import jax.numpy as jnp
from jax import lax
from jax.experimental import pallas as pl
from jax.experimental.pallas import tpu as pltpu
from jax.sharding import PartitionSpec as P

LX = 16
RING = 4
LINK_ROWS = 18
SMALL_ROWS = 80
NT = (((1,), (1,)), ((), ()))


def shift_matrix(moved_x, moved_y, sites):
    here = lax.broadcasted_iota(jnp.int32, (1, sites), 1)
    x, y = here % LX, here // LX
    rows = sites // LX
    there = ((y + moved_y + rows) % rows) * LX + (x + moved_x + LX) % LX
    source = lax.broadcasted_iota(jnp.int32, (sites, sites), 0)
    return jnp.where(source == there, 1.0, 0.0).astype(jnp.bfloat16)


def as_int(condition):
    return jnp.where(condition, 1, 0)


def times(one, two):
    return (one[0] * two[0] - one[1] * two[1], one[0] * two[1] + one[1] * two[0])


def plus(one, two):
    return (one[0] + two[0], one[1] + two[1])


def minus(one, two):
    return (one[0] - two[0], one[1] - two[1])


def kernel(scale, disp_hbm, rows_hbm, psi, links_hbm, out, disp, rows, links, g, sb, s32, u32, l32, w32, j32, x,
           perm, put, got, local_sem, halo_send, halo_recv, sum_send, sum_recv):
    me = lax.axis_index("site")
    core = lax.axis_index("ta") % 2
    after, behind = (me + 1) % RING, (me + RING - 1) % RING
    block = g.shape[4]
    sites = g.shape[5]

    fills = [
        pltpu.make_async_copy(psi.at[:, :, pl.ds(chunk * block, block), :], g.at[0, chunk], local_sem.at[chunk])
        for chunk in range(RING)
    ]
    fills.append(pltpu.make_async_copy(links_hbm, links, local_sem.at[RING]))
    fills.append(pltpu.make_async_copy(rows_hbm, rows, local_sem.at[RING + 1]))
    fills.append(pltpu.make_async_copy(disp_hbm, disp, local_sem.at[RING + 2]))
    for fill in fills:
        fill.start()
    barrier = pltpu.get_barrier_semaphore()
    for peer in (after, behind):
        pl.semaphore_signal(barrier, inc=1, device_id={"site": peer})
    pl.semaphore_wait(barrier, 2)
    for fill in fills:
        fill.wait()

    reader = (me + RING - 1 + 2 * core) % RING
    order = (2, 3, 1, 0)
    halo = []
    for number, offset in enumerate(order):
        sent = (reader + offset) % RING
        halo.append(pltpu.make_async_remote_copy(
            src_ref=g.at[0, sent], dst_ref=g.at[1, sent],
            send_sem=halo_send.at[number], recv_sem=halo_recv.at[number], device_id={"site": reader}))
    halo[0].start()

    s32[3 * LINK_ROWS:56] = jnp.zeros((56 - 3 * LINK_ROWS, sites), jnp.float32)
    for direction in range(3):
        for a in range(3):
            for b in range(3):
                at = direction * LINK_ROWS + (a * 3 + b) * 2
                s32[at:at + 2] = links[direction, a, b].astype(jnp.float32)
    vectors = RING * block
    number = lax.broadcasted_iota(jnp.int32, (24, vectors), 0)
    column = lax.broadcasted_iota(jnp.int32, (24, vectors), 1)
    wanted = jnp.zeros((24, vectors), jnp.int32)
    for i in range(4):
        wanted = jnp.where(number % 4 == i, rows[i], wanted)
    found = column == wanted
    picked = jnp.zeros((24, sites), jnp.float32)
    for q in range(2):
        for c in range(3):
            pick = jnp.where(found & (number // 4 == q * 3 + c), 1.0, 0.0).astype(jnp.bfloat16)
            whole = jnp.concatenate([g[0, chunk, q, c] for chunk in range(RING)], axis=0)
            picked += jnp.dot(pick, whole, preferred_element_type=jnp.float32)
    s32[56:80] = picked
    sb[0] = s32[...].astype(jnp.bfloat16)
    small = pltpu.make_async_remote_copy(
        src_ref=sb.at[0], dst_ref=sb.at[1],
        send_sem=halo_send.at[RING], recv_sem=halo_recv.at[RING], device_id={"site": reader})
    small.start()
    for copy in halo[1:]:
        copy.start()

    for m in range(2):
        d1, d2, d3 = disp[m, 0], disp[m, 1], disp[m, 2]
        back_x, back_y = as_int(d3 == 1), as_int(d3 == 2)
        perm[m, 0] = shift_matrix(-back_x, -back_y, sites)
        perm[m, 1] = shift_matrix(as_int(d2 == 1) - back_x, as_int(d2 == 2) - back_y, sites)
        perm[m, 2] = shift_matrix(as_int(d1 == 1) - back_x, as_int(d1 == 2) - back_y, sites)

    small.wait_recv()

    def imported(d):
        return (core + as_int(d == 3)) % 2 == 1

    def weights(m, carried):
        d1, d2, d3 = disp[m, 0], disp[m, 1], disp[m, 2]
        own, other = sb[0].astype(jnp.float32), sb[1].astype(jnp.float32)
        near = jnp.where(core == 1, other, own).astype(jnp.bfloat16)
        left = jnp.where(imported(d1), other, own)[56:80].astype(jnp.bfloat16)
        moved = jnp.dot(near, perm[m, 0], preferred_element_type=jnp.float32)
        entry = lax.broadcasted_iota(jnp.int32, (LINK_ROWS, sites), 0)
        identity = jnp.where((entry == 0) | (entry == 8) | (entry == 16), 1.0, 0.0)
        for k, d in enumerate((d1, d2, d3)):
            chosen = identity
            for direction in range(3):
                candidate = moved[direction * LINK_ROWS:(direction + 1) * LINK_ROWS]
                chosen = jnp.where(d == direction + 1, candidate, chosen)
            u32[k, 0:LINK_ROWS] = chosen
        l32[...] = scale * jnp.dot(left, perm[m, 2], preferred_element_type=jnp.float32)

        def link(k, a, b):
            at = (a * 3 + b) * 2
            return (u32[k, at:at + 1, :], u32[k, at + 1:at + 2, :])

        source = [(l32[4 * b:4 * b + 4, :], l32[12 + 4 * b:16 + 4 * b, :]) for b in range(3)]
        lefts = []
        for a in range(3):
            total = times(source[0], link(0, a, 0))
            for b in (1, 2):
                total = plus(total, times(source[b], link(0, a, b)))
            lefts.append(total)
        for d in range(3):
            triple = []
            for b in range(3):
                one, two = (b + 1) % 3, (b + 2) % 3
                triple.append(minus(times(lefts[two], link(2, one, d)), times(lefts[one], link(2, two, d))))
            for e in range(3):
                total = times(triple[0], link(1, 0, e))
                for b in (1, 2):
                    total = plus(total, times(triple[b], link(1, b, e)))
                w32[m, d, e, 0, 0:4, :] = total[0]
                w32[m, d, e, 1, 0:4, :] = total[1]
        return carried

    lax.fori_loop(0, 2, weights, 0)

    def build(slot, chunk):
        def one(m, carried):
            mine = g[0, chunk].reshape(6 * block, sites)
            theirs = g[1, chunk].reshape(6 * block, sites)
            mid = jnp.where(imported(disp[m, 1]), theirs, mine)
            j32[...] = jnp.dot(mid, perm[m, 1], preferred_element_type=jnp.float32).reshape(j32.shape)
            for half in range(sites // 128):
                lanes = slice(half * 128, half * 128 + 128)
                re = [j32[e, :, lanes] for e in range(3)]
                im = [j32[3 + e, :, lanes] for e in range(3)]
                for d in range(3):
                    for i in range(4):
                        total = None
                        for e in range(3):
                            w = (w32[m, d, e, 0, i:i + 1, lanes], w32[m, d, e, 1, i:i + 1, lanes])
                            term = times((re[e], im[e]), w)
                            total = term if total is None else plus(total, term)
                        place = slice(d * sites + half * 128, d * sites + half * 128 + 128)
                        for q in range(2):
                            x[m, slot, q, i * block:(i + 1) * block, place] = total[q].astype(jnp.bfloat16)
            return carried

        lax.fori_loop(0, 2, one, 0)

    for copy, offset in zip(halo, order):
        copy.wait_recv()
        build(offset, (me + offset) % RING)

    def contract(m, slots):
        far = (core + as_int(disp[m, 2] == 3)) % 2
        first, second = [], []
        for c in range(3):
            re = [g[far, chunk, 0, c] for chunk in range(RING)]
            im = [g[far, chunk, 1, c] for chunk in range(RING)]
            first.append(jnp.concatenate(re + im, axis=0))
            second.append(jnp.concatenate([-part for part in im] + re, axis=0))
        total = None
        for q, parts in enumerate((first, second)):
            left = jnp.concatenate([x[m, slot, q] for slot in slots], axis=0)
            product = lax.dot_general(
                left, jnp.concatenate(parts, axis=1), NT, preferred_element_type=jnp.float32)
            total = product if total is None else total + product
        rows_each = 4 * block
        return [total[k * rows_each:(k + 1) * rows_each].reshape(4, block, 2 * vectors) for k in range(2)]

    def carry(lane, step, source, peer):
        return pltpu.make_async_remote_copy(
            src_ref=put.at[lane, step], dst_ref=got.at[lane, step],
            send_sem=sum_send.at[lane, step], recv_sem=sum_recv.at[lane, step], device_id={"site": peer})

    up = [carry(0, step, None, after) for step in range(3)]
    down = [carry(1, step, None, behind) for step in range(3)]

    across, below = contract(0, (2, 3))
    put[0, 0] = across.astype(jnp.bfloat16)
    up[0].start()
    put[1, 1] = below.astype(jnp.bfloat16)
    across, above = contract(1, (2, 1))
    put[1, 0] = across.astype(jnp.bfloat16)
    down[0].start()
    put[0, 1] = above.astype(jnp.bfloat16)
    up[1].start()
    down[1].start()
    above, own = contract(0, (1, 0))
    out[0] = own
    up[0].wait_recv()
    put[0, 2] = (above + got[0, 0].astype(jnp.float32)).astype(jnp.bfloat16)
    up[2].start()
    below, own = contract(1, (3, 0))
    out[1] = own
    down[0].wait_recv()
    put[1, 2] = (below + got[1, 0].astype(jnp.float32)).astype(jnp.bfloat16)
    down[2].start()
    up[1].wait_recv()
    out[1] += got[0, 1].astype(jnp.float32)
    down[1].wait_recv()
    out[0] += got[1, 1].astype(jnp.float32)
    up[2].wait_recv()
    out[0] += got[0, 2].astype(jnp.float32)
    down[2].wait_recv()
    out[1] += got[1, 2].astype(jnp.float32)
    for copy in halo + [small] + up + down:
        copy.wait_send()


def on_device(eigenvectors, gauge_links, displacements, block_rows):
    psi = jnp.transpose(eigenvectors[:, :, :, 0, :], (0, 2, 1, 3))
    links = jnp.transpose(gauge_links[:, :, :, :, 0, :], (1, 2, 3, 0, 4))
    _, colors, vectors, sites = psi.shape
    block = vectors // RING
    scale = 1.0 / math.sqrt(24.0 * sites * RING)
    f32, bf16 = jnp.float32, jnp.bfloat16
    hbm = pl.BlockSpec(memory_space=pltpu.HBM)
    return pl.pallas_call(
        functools.partial(kernel, scale),
        out_shape=jax.ShapeDtypeStruct((2, 4, block, 2 * vectors), f32),
        in_specs=[hbm, hbm, hbm, hbm],
        out_specs=pl.BlockSpec(memory_space=pltpu.VMEM),
        scratch_shapes=[
            pltpu.SMEM(displacements.shape, displacements.dtype),
            pltpu.SMEM(block_rows.shape, block_rows.dtype),
            pltpu.VMEM(links.shape, bf16),
            pltpu.VMEM((2, RING, 2, 3, block, sites), bf16),
            pltpu.VMEM((2, SMALL_ROWS, sites), bf16),
            pltpu.VMEM((SMALL_ROWS, sites), f32),
            pltpu.VMEM((3, 24, sites), f32),
            pltpu.VMEM((24, sites), f32),
            pltpu.VMEM((2, 3, 3, 2, 8, sites), f32),
            pltpu.VMEM((6, block, sites), f32),
            pltpu.VMEM((2, RING, 2, 4 * block, 3 * sites), bf16),
            pltpu.VMEM((2, 3, sites, sites), bf16),
            pltpu.VMEM((2, 3, 4, block, 2 * vectors), bf16),
            pltpu.VMEM((2, 3, 4, block, 2 * vectors), bf16),
            pltpu.SemaphoreType.DMA((RING + 3,)),
            pltpu.SemaphoreType.DMA((RING + 1,)),
            pltpu.SemaphoreType.DMA((RING + 1,)),
            pltpu.SemaphoreType.DMA((2, 3)),
            pltpu.SemaphoreType.DMA((2, 3)),
        ],
        compiler_params=pltpu.CompilerParams(
            collective_id=0, has_side_effects=True, vmem_limit_bytes=63 * 1024 * 1024 + 512 * 1024),
    )(displacements, block_rows, psi, links)


def solution(mesh):
    return jax.shard_map(
        on_device,
        mesh=mesh,
        in_specs=(
            P("ta", None, None, "site", None),
            P("ta", None, None, None, "site", None),
            P(),
            P(),
        ),
        out_specs=P("ta", None, "site", None),
        check_vma=False,
    )
```

```python
import functools
import math

import jax
import jax.numpy as jnp
from jax import lax
from jax.experimental import pallas as pl
from jax.experimental.pallas import tpu as pltpu
from jax.sharding import PartitionSpec as P

LX = 16
RING = 4
LINK_ROWS = 18
TABLE_ROWS = 56
PARTS = 1
NT = (((1,), (1,)), ((), ()))


def shift_matrix(moved_x, moved_y, sites):
    here = lax.broadcasted_iota(jnp.int32, (1, sites), 1)
    x, y = here % LX, here // LX
    rows = sites // LX
    there = ((y + moved_y + rows) % rows) * LX + (x + moved_x + LX) % LX
    source = lax.broadcasted_iota(jnp.int32, (sites, sites), 0)
    return jnp.where(source == there, 1.0, 0.0).astype(jnp.bfloat16)


def as_int(condition):
    return jnp.where(condition, 1, 0)


def times(one, two):
    return (one[0] * two[0] - one[1] * two[1], one[0] * two[1] + one[1] * two[0])


def plus(one, two):
    return (one[0] + two[0], one[1] + two[1])


def minus(one, two):
    return (one[0] - two[0], one[1] - two[1])


def kernel(scale, disp_hbm, rows_hbm, psi, links_hbm, out, disp, rows, links, g, lb, kb, s32, u32, l32, w32, j32, x,
           perm, put, got, held, local_sem, halo_send, halo_recv, sum_send, sum_recv, ready):
    me = lax.axis_index("site")
    core = lax.axis_index("ta") % 2
    after, behind = (me + 1) % RING, (me + RING - 1) % RING
    block = g.shape[4]
    sites = g.shape[5]

    fills = [
        pltpu.make_async_copy(psi.at[:, :, pl.ds(chunk * block, block), :], g.at[0, chunk], local_sem.at[chunk])
        for chunk in range(RING)
    ]
    fills.append(pltpu.make_async_copy(links_hbm, links, local_sem.at[RING]))
    fills.append(pltpu.make_async_copy(rows_hbm, rows, local_sem.at[RING + 1]))
    fills.append(pltpu.make_async_copy(disp_hbm, disp, local_sem.at[RING + 2]))
    for fill in fills:
        fill.start()
    reader = (me + RING - 1 + 2 * core) % RING
    writer = (me + 1 + 2 * core) % RING
    barrier = pltpu.get_barrier_semaphore()
    pl.semaphore_signal(barrier, inc=1, device_id={"site": writer})
    pl.semaphore_wait(barrier, 1)
    pl.semaphore_signal(ready, inc=1, device_id={"site": reader})

    order = (2, 3, 1, 0)
    halo = []
    for number, offset in enumerate(order):
        sent = (reader + offset) % RING
        halo.append(pltpu.make_async_remote_copy(
            src_ref=psi.at[:, :, pl.ds(pl.multiple_of(sent * block, block), block), :], dst_ref=g.at[1, sent],
            send_sem=halo_send.at[number], recv_sem=halo_recv.at[number], device_id={"site": reader}))
    halo[0].start()
    for fill in fills:
        fill.wait()

    s32[3 * LINK_ROWS:] = jnp.zeros((TABLE_ROWS - 3 * LINK_ROWS, sites), jnp.float32)
    for direction in range(3):
        for a in range(3):
            for b in range(3):
                at = direction * LINK_ROWS + (a * 3 + b) * 2
                s32[at:at + 2] = links[direction, a, b].astype(jnp.float32)
    vectors = RING * block
    number = lax.broadcasted_iota(jnp.int32, (24, vectors), 0)
    column = lax.broadcasted_iota(jnp.int32, (24, vectors), 1)
    wanted = jnp.zeros((24, vectors), jnp.int32)
    for i in range(4):
        wanted = jnp.where(number % 4 == i, rows[i], wanted)
    found = column == wanted
    picked = jnp.zeros((24, sites), jnp.float32)
    for q in range(2):
        for c in range(3):
            pick = jnp.where(found & (number // 4 == q * 3 + c), 1.0, 0.0).astype(jnp.bfloat16)
            whole = jnp.concatenate([g[0, chunk, q, c] for chunk in range(RING)], axis=0)
            picked += jnp.dot(pick, whole, preferred_element_type=jnp.float32)
    lb[0] = picked.astype(jnp.bfloat16)
    kb[0] = s32[...].astype(jnp.bfloat16)
    small = [pltpu.make_async_remote_copy(
        src_ref=buffer.at[0], dst_ref=buffer.at[1],
        send_sem=halo_send.at[RING + number], recv_sem=halo_recv.at[RING + number], device_id={"site": reader})
        for number, buffer in enumerate((lb, kb))]
    small[0].start()

    @pl.when(core == 1)
    def _():
        small[1].start()

    for copy in halo[1:]:
        copy.start()

    for m in range(2):
        d1, d2, d3 = disp[m, 0], disp[m, 1], disp[m, 2]
        back_x, back_y = as_int(d3 == 1), as_int(d3 == 2)
        perm[m, 0] = shift_matrix(-back_x, -back_y, sites)
        perm[m, 1] = shift_matrix(as_int(d2 == 1) - back_x, as_int(d2 == 2) - back_y, sites)
        perm[m, 2] = shift_matrix(as_int(d1 == 1) - back_x, as_int(d1 == 2) - back_y, sites)

    small[0].wait_recv()

    @pl.when(core == 1)
    def _():
        small[1].wait_recv()

    def imported(d):
        return (core + as_int(d == 3)) % 2 == 1

    def weights(m, carried):
        d1, d2, d3 = disp[m, 0], disp[m, 1], disp[m, 2]
        moved = jnp.dot(kb[core], perm[m, 0], preferred_element_type=jnp.float32)
        left = lb[(core + as_int(d1 == 3)) % 2]
        entry = lax.broadcasted_iota(jnp.int32, (LINK_ROWS, sites), 0)
        identity = jnp.where((entry == 0) | (entry == 8) | (entry == 16), 1.0, 0.0)
        for k, d in enumerate((d1, d2, d3)):
            chosen = identity
            for direction in range(3):
                candidate = moved[direction * LINK_ROWS:(direction + 1) * LINK_ROWS]
                chosen = jnp.where(d == direction + 1, candidate, chosen)
            u32[k, 0:LINK_ROWS] = chosen
        l32[...] = scale * jnp.dot(left, perm[m, 2], preferred_element_type=jnp.float32)

        def link(k, a, b):
            at = (a * 3 + b) * 2
            return (u32[k, at:at + 1, :], u32[k, at + 1:at + 2, :])

        source = [(l32[4 * b:4 * b + 4, :], l32[12 + 4 * b:16 + 4 * b, :]) for b in range(3)]
        lefts = []
        for a in range(3):
            total = times(source[0], link(0, a, 0))
            for b in (1, 2):
                total = plus(total, times(source[b], link(0, a, b)))
            lefts.append(total)
        for d in range(3):
            triple = []
            for b in range(3):
                one, two = (b + 1) % 3, (b + 2) % 3
                triple.append(minus(times(lefts[two], link(2, one, d)), times(lefts[one], link(2, two, d))))
            for e in range(3):
                total = times(triple[0], link(1, 0, e))
                for b in (1, 2):
                    total = plus(total, times(triple[b], link(1, b, e)))
                w32[m, d, e, 0, 0:4, :] = total[0]
                w32[m, d, e, 1, 0:4, :] = total[1]
        return carried

    lax.fori_loop(0, 2, weights, 0)

    def build(slot, chunk):
        def one(m, carried):
            mine = g[0, chunk].reshape(6 * block, sites)
            theirs = g[1, chunk].reshape(6 * block, sites)
            mid = jnp.where(imported(disp[m, 1]), theirs, mine)
            j32[...] = jnp.dot(mid, perm[m, 1], preferred_element_type=jnp.float32).reshape(j32.shape)
            for half in range(sites // 128):
                lanes = slice(half * 128, half * 128 + 128)
                re = [j32[e, :, lanes] for e in range(3)]
                im = [j32[3 + e, :, lanes] for e in range(3)]
                for d in range(3):
                    for i in range(4):
                        total = None
                        for e in range(3):
                            w = (w32[m, d, e, 0, i:i + 1, lanes], w32[m, d, e, 1, i:i + 1, lanes])
                            term = times((re[e], im[e]), w)
                            total = term if total is None else plus(total, term)
                        place = slice(d * sites + half * 128, d * sites + half * 128 + 128)
                        for q in range(2):
                            x[m, slot, q, i * block:(i + 1) * block, place] = total[q].astype(jnp.bfloat16)
            return carried

        lax.fori_loop(0, 2, one, 0)

    for copy, offset in zip(halo, order):
        copy.wait_recv()
        if offset:
            build(offset, (me + offset) % RING)

    def contract(m, slots):
        far = (core + as_int(disp[m, 2] == 3)) % 2
        first, second = [], []
        for c in range(3):
            re = [g[far, chunk, 0, c] for chunk in range(RING)]
            im = [g[far, chunk, 1, c] for chunk in range(RING)]
            first.append(jnp.concatenate(re + im, axis=0))
            second.append(jnp.concatenate([-part for part in im] + re, axis=0))
        total = None
        for q, parts in enumerate((first, second)):
            left = jnp.concatenate([x[m, slot, q] for slot in slots], axis=0)
            product = lax.dot_general(
                left, jnp.concatenate(parts, axis=1), NT, preferred_element_type=jnp.float32)
            total = product if total is None else total + product
        rows_each = 4 * block
        return [total[k * rows_each:(k + 1) * rows_each].reshape(4, block, 2 * vectors) for k in range(len(slots))]

    def carry(lane, step, part, peer):
        rows_part = pl.ds(part * (4 // PARTS), 4 // PARTS)
        return pltpu.make_async_remote_copy(
            src_ref=put.at[lane, step, rows_part], dst_ref=got.at[lane, step, rows_part],
            send_sem=sum_send.at[lane, step, part], recv_sem=sum_recv.at[lane, step, part],
            device_id={"site": peer})

    up = [[carry(0, step, part, after) for part in range(PARTS)] for step in range(3)]
    down = [[carry(1, step, part, behind) for part in range(PARTS)] for step in range(3)]

    def send(copies):
        for copy in copies:
            copy.start()

    pl.semaphore_wait(ready, 1)
    across, = contract(0, (2,))
    put[0, 0] = across.astype(jnp.bfloat16)
    send(up[0])
    across, = contract(1, (2,))
    put[1, 0] = across.astype(jnp.bfloat16)
    send(down[0])
    above, = contract(1, (1,))
    put[0, 1] = above.astype(jnp.bfloat16)
    send(up[1])
    below, = contract(0, (3,))
    put[1, 1] = below.astype(jnp.bfloat16)
    send(down[1])
    build(0, me)
    above, own = contract(0, (1, 0))
    out[0] = own
    held[0] = above
    below, own = contract(1, (3, 0))
    out[1] = own
    held[1] = below
    each = 4 // PARTS
    for part in range(PARTS):
        these = slice(part * each, part * each + each)
        for lane, lines in ((0, up), (1, down)):
            lines[0][part].wait_recv()
            put[lane, 2, these] = (held[lane, these] + got[lane, 0, these].astype(jnp.float32)).astype(jnp.bfloat16)
            lines[2][part].start()
    for part in range(PARTS):
        these = slice(part * each, part * each + each)
        for lane, lines in ((0, up), (1, down)):
            lines[1][part].wait_recv()
            out[1 - lane, these] += got[lane, 1, these].astype(jnp.float32)
    for part in range(PARTS):
        these = slice(part * each, part * each + each)
        for lane, lines in ((0, up), (1, down)):
            lines[2][part].wait_recv()
            out[lane, these] += got[lane, 2, these].astype(jnp.float32)
    for copy in halo + small[:1]:
        copy.wait_send()
    for lines in up + down:
        for copy in lines:
            copy.wait_send()

    @pl.when(core == 1)
    def _():
        small[1].wait_send()


def on_device(eigenvectors, gauge_links, displacements, block_rows):
    psi = jnp.transpose(eigenvectors[:, :, :, 0, :], (0, 2, 1, 3))
    links = jnp.transpose(gauge_links[:, :, :, :, 0, :], (1, 2, 3, 0, 4))
    _, colors, vectors, sites = psi.shape
    block = vectors // RING
    scale = 1.0 / math.sqrt(24.0 * sites * RING)
    f32, bf16 = jnp.float32, jnp.bfloat16
    hbm = pl.BlockSpec(memory_space=pltpu.HBM)
    return pl.pallas_call(
        functools.partial(kernel, scale),
        out_shape=pltpu.VMEM((2, 4, block, 2 * vectors), f32),
        in_specs=[hbm, hbm, hbm, hbm],
        out_specs=pl.BlockSpec(memory_space=pltpu.VMEM),
        scratch_shapes=[
            pltpu.SMEM(displacements.shape, displacements.dtype),
            pltpu.SMEM(block_rows.shape, block_rows.dtype),
            pltpu.VMEM(links.shape, bf16),
            pltpu.VMEM((2, RING, 2, 3, block, sites), bf16),
            pltpu.VMEM((2, 24, sites), bf16),
            pltpu.VMEM((2, TABLE_ROWS, sites), bf16),
            pltpu.VMEM((TABLE_ROWS, sites), f32),
            pltpu.VMEM((3, 24, sites), f32),
            pltpu.VMEM((24, sites), f32),
            pltpu.VMEM((2, 3, 3, 2, 8, sites), f32),
            pltpu.VMEM((6, block, sites), f32),
            pltpu.VMEM((2, RING, 2, 4 * block, 3 * sites), bf16),
            pltpu.VMEM((2, 3, sites, sites), bf16),
            pltpu.VMEM((2, 3, 4, block, 2 * vectors), bf16),
            pltpu.VMEM((2, 3, 4, block, 2 * vectors), bf16),
            pltpu.VMEM((2, 4, block, 2 * vectors), f32),
            pltpu.SemaphoreType.DMA((RING + 3,)),
            pltpu.SemaphoreType.DMA((RING + 2,)),
            pltpu.SemaphoreType.DMA((RING + 2,)),
            pltpu.SemaphoreType.DMA((2, 3, PARTS)),
            pltpu.SemaphoreType.DMA((2, 3, PARTS)),
            pltpu.SemaphoreType.REGULAR,
        ],
        compiler_params=pltpu.CompilerParams(
            collective_id=0, has_side_effects=True, vmem_limit_bytes=62 * 1024 * 1024 + 512 * 1024),
    )(displacements, block_rows, psi, links)


def solution(mesh):
    return jax.shard_map(
        on_device,
        mesh=mesh,
        in_specs=(
            P("ta", None, None, "site", None),
            P("ta", None, None, None, "site", None),
            P(),
            P(),
        ),
        out_specs=P("ta", None, "site", None),
        check_vma=False,
    )
```

```python
import functools
import math

import jax
import jax.numpy as jnp
from jax import lax
from jax.experimental import pallas as pl
from jax.experimental.pallas import tpu as pltpu
from jax.sharding import PartitionSpec as P

LX = 16
RING = 4
LINK_ROWS = 18
TABLE_ROWS = 56
PARTS = 1
NT = (((1,), (1,)), ((), ()))


def shift_matrix(moved_x, moved_y, sites):
    here = lax.broadcasted_iota(jnp.int32, (1, sites), 1)
    x, y = here % LX, here // LX
    rows = sites // LX
    there = ((y + moved_y + rows) % rows) * LX + (x + moved_x + LX) % LX
    source = lax.broadcasted_iota(jnp.int32, (sites, sites), 0)
    return jnp.where(source == there, 1.0, 0.0).astype(jnp.bfloat16)


def as_int(condition):
    return jnp.where(condition, 1, 0)


def times(one, two):
    return (one[0] * two[0] - one[1] * two[1], one[0] * two[1] + one[1] * two[0])


def plus(one, two):
    return (one[0] + two[0], one[1] + two[1])


def minus(one, two):
    return (one[0] - two[0], one[1] - two[1])


def kernel(scale, disp_hbm, rows_hbm, psi, links_hbm, out, disp, rows, links, g, lb, kb, s32, u32, l32, w32, j32, x,
           perm, put, got, held, local_sem, halo_send, halo_recv, sum_send, sum_recv, ready):
    me = lax.axis_index("site")
    core = lax.axis_index("ta") % 2
    after, behind = (me + 1) % RING, (me + RING - 1) % RING
    block = g.shape[4]
    sites = g.shape[5]

    reader = (me + RING - 1 + 2 * core) % RING
    writer = (me + 1 + 2 * core) % RING
    barrier = pltpu.get_barrier_semaphore()
    pl.semaphore_signal(barrier, inc=1, device_id={"site": writer})

    fills = [
        pltpu.make_async_copy(psi.at[:, :, pl.ds(chunk * block, block), :], g.at[0, chunk], local_sem.at[chunk])
        for chunk in range(RING)
    ]
    fills.append(pltpu.make_async_copy(links_hbm, links, local_sem.at[RING]))
    fills.append(pltpu.make_async_copy(rows_hbm, rows, local_sem.at[RING + 1]))
    fills.append(pltpu.make_async_copy(disp_hbm, disp, local_sem.at[RING + 2]))
    for fill in fills:
        fill.start()
    for fill in fills:
        fill.wait()

    s32[3 * LINK_ROWS:] = jnp.zeros((TABLE_ROWS - 3 * LINK_ROWS, sites), jnp.float32)
    for direction in range(3):
        for a in range(3):
            for b in range(3):
                at = direction * LINK_ROWS + (a * 3 + b) * 2
                s32[at:at + 2] = links[direction, a, b].astype(jnp.float32)
    vectors = RING * block
    number = lax.broadcasted_iota(jnp.int32, (24, vectors), 0)
    column = lax.broadcasted_iota(jnp.int32, (24, vectors), 1)
    wanted = jnp.zeros((24, vectors), jnp.int32)
    for i in range(4):
        wanted = jnp.where(number % 4 == i, rows[i], wanted)
    found = column == wanted
    picked = jnp.zeros((24, sites), jnp.float32)
    for q in range(2):
        for c in range(3):
            pick = jnp.where(found & (number // 4 == q * 3 + c), 1.0, 0.0).astype(jnp.bfloat16)
            whole = jnp.concatenate([g[0, chunk, q, c] for chunk in range(RING)], axis=0)
            picked += jnp.dot(pick, whole, preferred_element_type=jnp.float32)
    lb[0] = picked.astype(jnp.bfloat16)
    kb[0] = s32[...].astype(jnp.bfloat16)
    pl.semaphore_wait(barrier, 1)
    pl.semaphore_signal(ready, inc=1, device_id={"site": reader})

    order = (2, 3, 1, 0)
    halo = []
    for number, offset in enumerate(order):
        sent = (reader + offset) % RING
        halo.append(pltpu.make_async_remote_copy(
            src_ref=psi.at[:, :, pl.ds(pl.multiple_of(sent * block, block), block), :], dst_ref=g.at[1, sent],
            send_sem=halo_send.at[number], recv_sem=halo_recv.at[number], device_id={"site": reader}))

    small = [pltpu.make_async_remote_copy(
        src_ref=buffer.at[0], dst_ref=buffer.at[1],
        send_sem=halo_send.at[RING + number], recv_sem=halo_recv.at[RING + number], device_id={"site": reader})
        for number, buffer in enumerate((lb, kb))]
    small[0].start()

    @pl.when(core == 1)
    def _():
        small[1].start()

    for copy in halo:
        copy.start()

    for m in range(2):
        d1, d2, d3 = disp[m, 0], disp[m, 1], disp[m, 2]
        back_x, back_y = as_int(d3 == 1), as_int(d3 == 2)
        perm[m, 0] = shift_matrix(-back_x, -back_y, sites)
        perm[m, 1] = shift_matrix(as_int(d2 == 1) - back_x, as_int(d2 == 2) - back_y, sites)
        perm[m, 2] = shift_matrix(as_int(d1 == 1) - back_x, as_int(d1 == 2) - back_y, sites)

    small[0].wait_recv()

    @pl.when(core == 1)
    def _():
        small[1].wait_recv()

    def imported(d):
        return (core + as_int(d == 3)) % 2 == 1

    def weights(m, carried):
        d1, d2, d3 = disp[m, 0], disp[m, 1], disp[m, 2]
        moved = jnp.dot(kb[core], perm[m, 0], preferred_element_type=jnp.float32)
        left = lb[(core + as_int(d1 == 3)) % 2]
        entry = lax.broadcasted_iota(jnp.int32, (LINK_ROWS, sites), 0)
        identity = jnp.where((entry == 0) | (entry == 8) | (entry == 16), 1.0, 0.0)
        for k, d in enumerate((d1, d2, d3)):
            chosen = identity
            for direction in range(3):
                candidate = moved[direction * LINK_ROWS:(direction + 1) * LINK_ROWS]
                chosen = jnp.where(d == direction + 1, candidate, chosen)
            u32[k, 0:LINK_ROWS] = chosen
        l32[...] = scale * jnp.dot(left, perm[m, 2], preferred_element_type=jnp.float32)

        def link(k, a, b):
            at = (a * 3 + b) * 2
            return (u32[k, at:at + 1, :], u32[k, at + 1:at + 2, :])

        source = [(l32[4 * b:4 * b + 4, :], l32[12 + 4 * b:16 + 4 * b, :]) for b in range(3)]
        lefts = []
        for a in range(3):
            total = times(source[0], link(0, a, 0))
            for b in (1, 2):
                total = plus(total, times(source[b], link(0, a, b)))
            lefts.append(total)
        for d in range(3):
            triple = []
            for b in range(3):
                one, two = (b + 1) % 3, (b + 2) % 3
                triple.append(minus(times(lefts[two], link(2, one, d)), times(lefts[one], link(2, two, d))))
            for e in range(3):
                total = times(triple[0], link(1, 0, e))
                for b in (1, 2):
                    total = plus(total, times(triple[b], link(1, b, e)))
                w32[m, d, e, 0, 0:4, :] = total[0]
                w32[m, d, e, 1, 0:4, :] = total[1]
        return carried

    lax.fori_loop(0, 2, weights, 0)

    def build(slot, chunk):
        def one(m, carried):
            mine = g[0, chunk].reshape(6 * block, sites)
            theirs = g[1, chunk].reshape(6 * block, sites)
            mid = jnp.where(imported(disp[m, 1]), theirs, mine)
            j32[...] = jnp.dot(mid, perm[m, 1], preferred_element_type=jnp.float32).reshape(j32.shape)
            for half in range(sites // 128):
                lanes = slice(half * 128, half * 128 + 128)
                re = [j32[e, :, lanes] for e in range(3)]
                im = [j32[3 + e, :, lanes] for e in range(3)]
                for d in range(3):
                    for i in range(4):
                        total = None
                        for e in range(3):
                            w = (w32[m, d, e, 0, i:i + 1, lanes], w32[m, d, e, 1, i:i + 1, lanes])
                            term = times((re[e], im[e]), w)
                            total = term if total is None else plus(total, term)
                        place = slice(d * sites + half * 128, d * sites + half * 128 + 128)
                        for q in range(2):
                            x[m, slot, q, i * block:(i + 1) * block, place] = total[q].astype(jnp.bfloat16)
            return carried

        lax.fori_loop(0, 2, one, 0)

    for copy, offset in zip(halo, order):
        copy.wait_recv()
        if offset:
            build(offset, (me + offset) % RING)

    def contract(m, slots):
        far = (core + as_int(disp[m, 2] == 3)) % 2
        first, second = [], []
        for c in range(3):
            re = [g[far, chunk, 0, c] for chunk in range(RING)]
            im = [g[far, chunk, 1, c] for chunk in range(RING)]
            first.append(jnp.concatenate(re + im, axis=0))
            second.append(jnp.concatenate([-part for part in im] + re, axis=0))
        total = None
        for q, parts in enumerate((first, second)):
            left = jnp.concatenate([x[m, slot, q] for slot in slots], axis=0)
            product = lax.dot_general(
                left, jnp.concatenate(parts, axis=1), NT, preferred_element_type=jnp.float32)
            total = product if total is None else total + product
        rows_each = 4 * block
        return [total[k * rows_each:(k + 1) * rows_each].reshape(4, block, 2 * vectors) for k in range(len(slots))]

    def carry(lane, step, part, peer):
        rows_part = pl.ds(part * (4 // PARTS), 4 // PARTS)
        return pltpu.make_async_remote_copy(
            src_ref=put.at[lane, step, rows_part], dst_ref=got.at[lane, step, rows_part],
            send_sem=sum_send.at[lane, step, part], recv_sem=sum_recv.at[lane, step, part],
            device_id={"site": peer})

    up = [[carry(0, step, part, after) for part in range(PARTS)] for step in range(3)]
    down = [[carry(1, step, part, behind) for part in range(PARTS)] for step in range(3)]

    def send(copies):
        for copy in copies:
            copy.start()

    pl.semaphore_wait(ready, 1)
    across, = contract(0, (2,))
    put[0, 0] = across.astype(jnp.bfloat16)
    send(up[0])
    across, = contract(1, (2,))
    put[1, 0] = across.astype(jnp.bfloat16)
    send(down[0])
    above, = contract(1, (1,))
    put[0, 1] = above.astype(jnp.bfloat16)
    send(up[1])
    below, = contract(0, (3,))
    put[1, 1] = below.astype(jnp.bfloat16)
    send(down[1])
    build(0, me)
    above, own = contract(0, (1, 0))
    out[0] = own
    held[0] = above
    below, own = contract(1, (3, 0))
    out[1] = own
    held[1] = below
    each = 4 // PARTS
    for part in range(PARTS):
        these = slice(part * each, part * each + each)
        for lane, lines in ((0, up), (1, down)):
            lines[0][part].wait_recv()
            put[lane, 2, these] = (held[lane, these] + got[lane, 0, these].astype(jnp.float32)).astype(jnp.bfloat16)
            lines[2][part].start()
    for part in range(PARTS):
        these = slice(part * each, part * each + each)
        for lane, lines in ((0, up), (1, down)):
            lines[1][part].wait_recv()
            out[1 - lane, these] += got[lane, 1, these].astype(jnp.float32)
    for part in range(PARTS):
        these = slice(part * each, part * each + each)
        for lane, lines in ((0, up), (1, down)):
            lines[2][part].wait_recv()
            out[lane, these] += got[lane, 2, these].astype(jnp.float32)
    for copy in halo + small[:1]:
        copy.wait_send()
    for lines in up + down:
        for copy in lines:
            copy.wait_send()

    @pl.when(core == 1)
    def _():
        small[1].wait_send()


def on_device(eigenvectors, gauge_links, displacements, block_rows):
    psi = jnp.transpose(eigenvectors[:, :, :, 0, :], (0, 2, 1, 3))
    links = jnp.transpose(gauge_links[:, :, :, :, 0, :], (1, 2, 3, 0, 4))
    _, colors, vectors, sites = psi.shape
    block = vectors // RING
    scale = 1.0 / math.sqrt(24.0 * sites * RING)
    f32, bf16 = jnp.float32, jnp.bfloat16
    hbm = pl.BlockSpec(memory_space=pltpu.HBM)
    return pl.pallas_call(
        functools.partial(kernel, scale),
        out_shape=pltpu.VMEM((2, 4, block, 2 * vectors), f32),
        in_specs=[hbm, hbm, hbm, hbm],
        out_specs=pl.BlockSpec(memory_space=pltpu.VMEM),
        scratch_shapes=[
            pltpu.SMEM(displacements.shape, displacements.dtype),
            pltpu.SMEM(block_rows.shape, block_rows.dtype),
            pltpu.VMEM(links.shape, bf16),
            pltpu.VMEM((2, RING, 2, 3, block, sites), bf16),
            pltpu.VMEM((2, 24, sites), bf16),
            pltpu.VMEM((2, TABLE_ROWS, sites), bf16),
            pltpu.VMEM((TABLE_ROWS, sites), f32),
            pltpu.VMEM((3, 24, sites), f32),
            pltpu.VMEM((24, sites), f32),
            pltpu.VMEM((2, 3, 3, 2, 8, sites), f32),
            pltpu.VMEM((6, block, sites), f32),
            pltpu.VMEM((2, RING, 2, 4 * block, 3 * sites), bf16),
            pltpu.VMEM((2, 3, sites, sites), bf16),
            pltpu.VMEM((2, 3, 4, block, 2 * vectors), bf16),
            pltpu.VMEM((2, 3, 4, block, 2 * vectors), bf16),
            pltpu.VMEM((2, 4, block, 2 * vectors), f32),
            pltpu.SemaphoreType.DMA((RING + 3,)),
            pltpu.SemaphoreType.DMA((RING + 2,)),
            pltpu.SemaphoreType.DMA((RING + 2,)),
            pltpu.SemaphoreType.DMA((2, 3, PARTS)),
            pltpu.SemaphoreType.DMA((2, 3, PARTS)),
            pltpu.SemaphoreType.REGULAR,
        ],
        compiler_params=pltpu.CompilerParams(
            collective_id=0, has_side_effects=True, vmem_limit_bytes=62 * 1024 * 1024 + 512 * 1024),
    )(displacements, block_rows, psi, links)


def solution(mesh):
    return jax.shard_map(
        on_device,
        mesh=mesh,
        in_specs=(
            P("ta", None, None, "site", None),
            P("ta", None, None, None, "site", None),
            P(),
            P(),
        ),
        out_specs=P("ta", None, "site", None),
        check_vma=False,
    )
```

```python
import functools
import math

import jax
import jax.numpy as jnp
from jax import lax
from jax.experimental import pallas as pl
from jax.experimental.pallas import tpu as pltpu
from jax.sharding import PartitionSpec as P

LX = 16
RING = 4
LINK_ROWS = 18
TABLE_ROWS = 56
PARTS = 1
NT = (((1,), (1,)), ((), ()))


def shift_matrix(moved_x, moved_y, sites):
    here = lax.broadcasted_iota(jnp.int32, (1, sites), 1)
    x, y = here % LX, here // LX
    rows = sites // LX
    there = ((y + moved_y + rows) % rows) * LX + (x + moved_x + LX) % LX
    source = lax.broadcasted_iota(jnp.int32, (sites, sites), 0)
    return jnp.where(source == there, 1.0, 0.0).astype(jnp.bfloat16)


def as_int(condition):
    return jnp.where(condition, 1, 0)


def times(one, two):
    return (one[0] * two[0] - one[1] * two[1], one[0] * two[1] + one[1] * two[0])


def plus(one, two):
    return (one[0] + two[0], one[1] + two[1])


def minus(one, two):
    return (one[0] - two[0], one[1] - two[1])


def kernel(scale, disp_hbm, rows_hbm, psi, links_hbm, out, disp, rows, links, g, lb, kb, s32, u32, l32, w32, j32, x,
           perm, put, got, held, local_sem, halo_send, halo_recv, sum_send, sum_recv, ready):
    me = lax.axis_index("site")
    core = lax.axis_index("ta") % 2
    after, behind = (me + 1) % RING, (me + RING - 1) % RING
    block = g.shape[4]
    sites = g.shape[5]

    reader = (me + RING - 1 + 2 * core) % RING
    writer = (me + 1 + 2 * core) % RING
    barrier = pltpu.get_barrier_semaphore()
    pl.semaphore_signal(barrier, inc=1, device_id={"site": writer})

    fills = [
        pltpu.make_async_copy(psi.at[:, :, pl.ds(chunk * block, block), :], g.at[0, chunk], local_sem.at[chunk])
        for chunk in range(RING)
    ]
    fills.append(pltpu.make_async_copy(links_hbm, links.at[0], local_sem.at[RING]))
    fills.append(pltpu.make_async_copy(rows_hbm, rows, local_sem.at[RING + 1]))
    fills.append(pltpu.make_async_copy(disp_hbm, disp, local_sem.at[RING + 2]))
    for fill in fills:
        fill.start()
    for fill in fills:
        fill.wait()

    vectors = RING * block
    number = lax.broadcasted_iota(jnp.int32, (24, vectors), 0)
    column = lax.broadcasted_iota(jnp.int32, (24, vectors), 1)
    wanted = jnp.zeros((24, vectors), jnp.int32)
    for i in range(4):
        wanted = jnp.where(number % 4 == i, rows[i], wanted)
    found = column == wanted
    picked = jnp.zeros((24, sites), jnp.float32)
    for q in range(2):
        for c in range(3):
            pick = jnp.where(found & (number // 4 == q * 3 + c), 1.0, 0.0).astype(jnp.bfloat16)
            whole = jnp.concatenate([g[0, chunk, q, c] for chunk in range(RING)], axis=0)
            picked += jnp.dot(pick, whole, preferred_element_type=jnp.float32)
    lb[0] = picked.astype(jnp.bfloat16)
    pl.semaphore_wait(barrier, 1)
    pl.semaphore_signal(ready, inc=1, device_id={"site": reader})

    order = (2, 3, 1, 0)
    halo = []
    for number, offset in enumerate(order):
        sent = (reader + offset) % RING
        halo.append(pltpu.make_async_remote_copy(
            src_ref=g.at[0, sent], dst_ref=g.at[1, sent],
            send_sem=halo_send.at[number], recv_sem=halo_recv.at[number], device_id={"site": reader}))

    small = [pltpu.make_async_remote_copy(
        src_ref=buffer.at[0], dst_ref=buffer.at[1],
        send_sem=halo_send.at[RING + number], recv_sem=halo_recv.at[RING + number], device_id={"site": reader})
        for number, buffer in enumerate((lb, links))]
    small[0].start()

    @pl.when(core == 1)
    def _():
        small[1].start()

    for copy in halo:
        copy.start()

    for m in range(2):
        d1, d2, d3 = disp[m, 0], disp[m, 1], disp[m, 2]
        back_x, back_y = as_int(d3 == 1), as_int(d3 == 2)
        perm[m, 0] = shift_matrix(-back_x, -back_y, sites)
        perm[m, 1] = shift_matrix(as_int(d2 == 1) - back_x, as_int(d2 == 2) - back_y, sites)
        perm[m, 2] = shift_matrix(as_int(d1 == 1) - back_x, as_int(d1 == 2) - back_y, sites)

    small[0].wait_recv()

    @pl.when(core == 1)
    def _():
        small[1].wait_recv()

    s32[3 * LINK_ROWS:] = jnp.zeros((TABLE_ROWS - 3 * LINK_ROWS, sites), jnp.float32)
    for direction in range(3):
        for a in range(3):
            for b in range(3):
                at = direction * LINK_ROWS + (a * 3 + b) * 2
                s32[at:at + 2] = links[core, direction, a, b].astype(jnp.float32)
    kb[...] = s32[...].astype(jnp.bfloat16)

    def imported(d):
        return (core + as_int(d == 3)) % 2 == 1

    def weights(m, carried):
        d1, d2, d3 = disp[m, 0], disp[m, 1], disp[m, 2]
        moved = jnp.dot(kb[...], perm[m, 0], preferred_element_type=jnp.float32)
        left = lb[(core + as_int(d1 == 3)) % 2]
        entry = lax.broadcasted_iota(jnp.int32, (LINK_ROWS, sites), 0)
        identity = jnp.where((entry == 0) | (entry == 8) | (entry == 16), 1.0, 0.0)
        for k, d in enumerate((d1, d2, d3)):
            chosen = identity
            for direction in range(3):
                candidate = moved[direction * LINK_ROWS:(direction + 1) * LINK_ROWS]
                chosen = jnp.where(d == direction + 1, candidate, chosen)
            u32[k, 0:LINK_ROWS] = chosen
        l32[...] = scale * jnp.dot(left, perm[m, 2], preferred_element_type=jnp.float32)

        def link(k, a, b):
            at = (a * 3 + b) * 2
            return (u32[k, at:at + 1, :], u32[k, at + 1:at + 2, :])

        source = [(l32[4 * b:4 * b + 4, :], l32[12 + 4 * b:16 + 4 * b, :]) for b in range(3)]
        lefts = []
        for a in range(3):
            total = times(source[0], link(0, a, 0))
            for b in (1, 2):
                total = plus(total, times(source[b], link(0, a, b)))
            lefts.append(total)
        for d in range(3):
            triple = []
            for b in range(3):
                one, two = (b + 1) % 3, (b + 2) % 3
                triple.append(minus(times(lefts[two], link(2, one, d)), times(lefts[one], link(2, two, d))))
            for e in range(3):
                total = times(triple[0], link(1, 0, e))
                for b in (1, 2):
                    total = plus(total, times(triple[b], link(1, b, e)))
                w32[m, d, e, 0, 0:4, :] = total[0]
                w32[m, d, e, 1, 0:4, :] = total[1]
        return carried

    lax.fori_loop(0, 2, weights, 0)

    def build(slot, chunk):
        def one(m, carried):
            mine = g[0, chunk].reshape(6 * block, sites)
            theirs = g[1, chunk].reshape(6 * block, sites)
            mid = jnp.where(imported(disp[m, 1]), theirs, mine)
            j32[...] = jnp.dot(mid, perm[m, 1], preferred_element_type=jnp.float32).reshape(j32.shape)
            for half in range(sites // 128):
                lanes = slice(half * 128, half * 128 + 128)
                re = [j32[e, :, lanes] for e in range(3)]
                im = [j32[3 + e, :, lanes] for e in range(3)]
                for d in range(3):
                    for i in range(4):
                        total = None
                        for e in range(3):
                            w = (w32[m, d, e, 0, i:i + 1, lanes], w32[m, d, e, 1, i:i + 1, lanes])
                            term = times((re[e], im[e]), w)
                            total = term if total is None else plus(total, term)
                        place = slice(d * sites + half * 128, d * sites + half * 128 + 128)
                        for q in range(2):
                            x[m, slot, q, i * block:(i + 1) * block, place] = total[q].astype(jnp.bfloat16)
            return carried

        lax.fori_loop(0, 2, one, 0)

    for copy, offset in zip(halo, order):
        copy.wait_recv()
        if offset:
            build(offset, (me + offset) % RING)

    def contract(m, slots):
        far = (core + as_int(disp[m, 2] == 3)) % 2
        first, second = [], []
        for c in range(3):
            re = [g[far, chunk, 0, c] for chunk in range(RING)]
            im = [g[far, chunk, 1, c] for chunk in range(RING)]
            first.append(jnp.concatenate(re + im, axis=0))
            second.append(jnp.concatenate([-part for part in im] + re, axis=0))
        total = None
        for q, parts in enumerate((first, second)):
            left = jnp.concatenate([x[m, slot, q] for slot in slots], axis=0)
            product = lax.dot_general(
                left, jnp.concatenate(parts, axis=1), NT, preferred_element_type=jnp.float32)
            total = product if total is None else total + product
        rows_each = 4 * block
        return [total[k * rows_each:(k + 1) * rows_each].reshape(4, block, 2 * vectors) for k in range(len(slots))]

    def carry(lane, step, part, peer):
        rows_part = pl.ds(part * (4 // PARTS), 4 // PARTS)
        return pltpu.make_async_remote_copy(
            src_ref=put.at[lane, step, rows_part], dst_ref=got.at[lane, step, rows_part],
            send_sem=sum_send.at[lane, step, part], recv_sem=sum_recv.at[lane, step, part],
            device_id={"site": peer})

    up = [[carry(0, step, part, after) for part in range(PARTS)] for step in range(3)]
    down = [[carry(1, step, part, behind) for part in range(PARTS)] for step in range(3)]

    def send(copies):
        for copy in copies:
            copy.start()

    pl.semaphore_wait(ready, 1)
    across, = contract(0, (2,))
    put[0, 0] = across.astype(jnp.bfloat16)
    send(up[0])
    across, = contract(1, (2,))
    put[1, 0] = across.astype(jnp.bfloat16)
    send(down[0])
    above, = contract(1, (1,))
    put[0, 1] = above.astype(jnp.bfloat16)
    send(up[1])
    below, = contract(0, (3,))
    put[1, 1] = below.astype(jnp.bfloat16)
    send(down[1])
    build(0, me)
    above, own = contract(0, (1, 0))
    out[0] = own
    held[0] = above
    below, own = contract(1, (3, 0))
    out[1] = own
    held[1] = below
    each = 4 // PARTS
    for part in range(PARTS):
        these = slice(part * each, part * each + each)
        for lane, lines in ((0, up), (1, down)):
            lines[0][part].wait_recv()
            put[lane, 2, these] = (held[lane, these] + got[lane, 0, these].astype(jnp.float32)).astype(jnp.bfloat16)
            lines[2][part].start()
    for part in range(PARTS):
        these = slice(part * each, part * each + each)
        for lane, lines in ((0, up), (1, down)):
            lines[1][part].wait_recv()
            out[1 - lane, these] += got[lane, 1, these].astype(jnp.float32)
    for part in range(PARTS):
        these = slice(part * each, part * each + each)
        for lane, lines in ((0, up), (1, down)):
            lines[2][part].wait_recv()
            out[lane, these] += got[lane, 2, these].astype(jnp.float32)
    for copy in halo + small[:1]:
        copy.wait_send()
    for lines in up + down:
        for copy in lines:
            copy.wait_send()

    @pl.when(core == 1)
    def _():
        small[1].wait_send()


def on_device(eigenvectors, gauge_links, displacements, block_rows):
    psi = jnp.transpose(eigenvectors[:, :, :, 0, :], (0, 2, 1, 3))
    links = jnp.transpose(gauge_links[:, :, :, :, 0, :], (1, 2, 3, 0, 4))
    _, colors, vectors, sites = psi.shape
    block = vectors // RING
    scale = 1.0 / math.sqrt(24.0 * sites * RING)
    f32, bf16 = jnp.float32, jnp.bfloat16
    hbm = pl.BlockSpec(memory_space=pltpu.HBM)
    return pl.pallas_call(
        functools.partial(kernel, scale),
        out_shape=pltpu.VMEM((2, 4, block, 2 * vectors), f32),
        in_specs=[hbm, hbm, hbm, hbm],
        out_specs=pl.BlockSpec(memory_space=pltpu.VMEM),
        scratch_shapes=[
            pltpu.SMEM(displacements.shape, displacements.dtype),
            pltpu.SMEM(block_rows.shape, block_rows.dtype),
            pltpu.VMEM((2,) + links.shape, bf16),
            pltpu.VMEM((2, RING, 2, 3, block, sites), bf16),
            pltpu.VMEM((2, 24, sites), bf16),
            pltpu.VMEM((TABLE_ROWS, sites), bf16),
            pltpu.VMEM((TABLE_ROWS, sites), f32),
            pltpu.VMEM((3, 24, sites), f32),
            pltpu.VMEM((24, sites), f32),
            pltpu.VMEM((2, 3, 3, 2, 8, sites), f32),
            pltpu.VMEM((6, block, sites), f32),
            pltpu.VMEM((2, RING, 2, 4 * block, 3 * sites), bf16),
            pltpu.VMEM((2, 3, sites, sites), bf16),
            pltpu.VMEM((2, 3, 4, block, 2 * vectors), bf16),
            pltpu.VMEM((2, 3, 4, block, 2 * vectors), bf16),
            pltpu.VMEM((2, 4, block, 2 * vectors), f32),
            pltpu.SemaphoreType.DMA((RING + 3,)),
            pltpu.SemaphoreType.DMA((RING + 2,)),
            pltpu.SemaphoreType.DMA((RING + 2,)),
            pltpu.SemaphoreType.DMA((2, 3, PARTS)),
            pltpu.SemaphoreType.DMA((2, 3, PARTS)),
            pltpu.SemaphoreType.REGULAR,
        ],
        compiler_params=pltpu.CompilerParams(
            collective_id=0, has_side_effects=True, vmem_limit_bytes=62 * 1024 * 1024 + 512 * 1024),
    )(displacements, block_rows, psi, links)


def solution(mesh):
    return jax.shard_map(
        on_device,
        mesh=mesh,
        in_specs=(
            P("ta", None, None, "site", None),
            P("ta", None, None, None, "site", None),
            P(),
            P(),
        ),
        out_specs=P("ta", None, "site", None),
        check_vma=False,
    )
```
